32 devices in a mesh: xy: 8 (over y, x, core), gz: 4 (over z).
Axes of the slice: x: 2, y: 2, z: 4, core: 2. Of those that a mesh axis runs over, the one named last changes fastest.
Arguments:
- features: bfloat16 [8, 2, 4, 64, 128], P('xy', None, 'gz'), may hold values from -6 to 6
- cotangent: bfloat16 [8, 2, 4, 64, 128], P('xy', None, 'gz'), may hold values from -6 to 6
- positions: float32 [8, 2, 4, 3, 64], P('xy', None, 'gz'), may hold values from 0 to 1
- counts: int32 [8, 2, 4], P('xy', None, 'gz'), may hold values from 32 to 64
- neighbour_mask: int32 [8, 2, 4, 27], P('xy', None, 'gz'), may hold values 0 or 1
- proj_weight: bfloat16 [128, 64], replicated, may hold values from -0.5 to 0.5
- out_weight: bfloat16 [64, 128], replicated, may hold values from -0.75 to 0.75
- radial_weight: float32 [8, 64], replicated, may hold values from -58 to 58
Outputs:
- updated: bfloat16 [8, 2, 4, 64, 128], P('xy', None, 'gz')
- feature_grad: bfloat16 [8, 2, 4, 64, 128], P('xy', None, 'gz')
The draws below stay inside these ranges and needn't reach their ends.
Inputs may be any that keep to these rules, and one draw needn't show every extreme that they name: `counts`: the atoms of a cell beyond its count are padding. `neighbour_mask`: entry d refers to the direction numbered as in the reference program.
All inputs are finite; a program needn't handle non-finite values. No bound on the sum of `neighbour_mask` on one device may be relied on, other than what follows from the above.
Results may differ from the reference program's by a relative error of at most 0.007.
Values may be sent and summed in bfloat16 or wider, within the bound.
A program may use at most 64 MiB of HBM per device.

```python
import jax
import jax.numpy as jnp
from jax import lax

ATOMS = 64
CH = 128
PROJ = 64
BASES = 8
NX = 8
NY = 2
NZ = 4


def draw_radial_weight(key, part):
    centres = (jnp.arange(BASES, dtype=jnp.float32) + 0.5) / BASES
    damping = jnp.maximum(jnp.square(1.0 - centres), 1.0 / 64.0)
    row_scale = (0.3 / damping)[:, None]
    sample = jax.random.truncated_normal(key, -3.0, 3.0, (BASES, PROJ), jnp.float32)
    return (sample * row_scale).astype(jnp.float32)


def with_ends(entries, rng, smallest, top_value):
    extent = entries.shape
    place = [jax.random.randint(jax.random.fold_in(rng, axis), (), 0, extent[axis]) for axis in range(len(extent))]
    entries = entries.at[tuple(place)].set(smallest)
    longest = extent.index(max(extent))
    place[longest] = (place[longest] + 1) % extent[longest]
    return entries.at[tuple(place)].set(top_value)


def block_scale(rng, dims, split, smallest, high):
    def one(axis_at, shards_of):
        steps = jax.random.uniform(jax.random.fold_in(jax.random.fold_in(rng, 6), axis_at), (shards_of,), jnp.float32, smallest / len(split), high / len(split))
        return jnp.repeat(jnp.exp(steps), dims[axis_at] // shards_of).reshape((-1,) + (1,) * (len(dims) - axis_at - 1))

    loudness = one(*split[0])
    for cut in split[1:]:
        loudness = loudness * one(*cut)
    return loudness


def centred(rng, dims, deviation, bound, pieces=(), kind=jnp.bfloat16):
    gain = block_scale(rng, dims, pieces, -0.22, 0.18) if pieces else 1.0
    entries = jax.random.normal(rng, dims, jnp.float32) * deviation * gain
    return jnp.minimum(jnp.maximum(entries, -bound), bound).astype(kind)


def setup_inputs(seed: int = 0) -> dict:
    arg_keys = jax.random.split(jax.random.key(seed), 9)
    features = centred(arg_keys[0], (NX, NY, NZ, ATOMS, CH), 1.0, 6.0, ((0, 8), (2, 4)))
    cotangent = centred(arg_keys[1], (NX, NY, NZ, ATOMS, CH), 1.0, 6.0, ((0, 8), (2, 4)))
    positions = jnp.clip(1.0 * jax.random.uniform(arg_keys[2], (NX, NY, NZ, 3, ATOMS), jnp.float32) ** block_scale(arg_keys[2], (NX, NY, NZ, 3, ATOMS), ((0, 8), (2, 4)), -0.2, 0.2), 0.0, 1.0)
    counts = with_ends(jax.random.randint(arg_keys[3], (NX, NY, NZ), ATOMS // 2, ATOMS + 1), jax.random.fold_in(arg_keys[3], 1), ATOMS // 2, ATOMS).astype(jnp.int32)
    neighbour_mask = with_ends((jax.random.randint(arg_keys[4], (NX, NY, NZ, 27), 0, 8) < 7).astype(jnp.int32), jax.random.fold_in(arg_keys[4], 1), 0, 1)
    proj_weight = centred(arg_keys[5], (CH, PROJ), CH ** -0.5, 0.5)
    out_weight = centred(arg_keys[6], (PROJ, CH), PROJ ** -0.5, 0.75)
    radial_weight = draw_radial_weight(jax.random.fold_in(arg_keys[8], 71), 0)
    return {"features": features, "cotangent": cotangent, "positions": positions, "counts": counts, "neighbour_mask": neighbour_mask, "proj_weight": proj_weight, "out_weight": out_weight, "radial_weight": radial_weight}


def offsets():
    return [(direction // 9 - 1, (direction // 3) % 3 - 1, direction % 3 - 1) for direction in range(27)]


def build_tiles(own_pos, own_valid, other_pos, other_valid, cell_gate, shift_vec, self_flag):
    separation = other_pos[:, :, None, :] + shift_vec[None, :, None, None] - own_pos[:, :, :, None]
    squared = 4.0 * jnp.sum(separation * separation, axis=1)
    atom_count = own_pos.shape[2]
    diagonal_ones = (jnp.arange(atom_count)[:, None] == jnp.arange(atom_count)[None, :]).astype(jnp.float32)
    pair_keep = own_valid[:, :, None] * other_valid[:, None, :] * cell_gate[:, None, None]
    pair_keep = pair_keep * (1.0 - self_flag * diagonal_ones)
    envelope = jnp.square(jnp.maximum(1.0 - squared, 0.0)) * pair_keep
    basis_list = [(envelope * jnp.exp(-2.0 * jnp.square(BASES * squared - which_basis - 0.5))).astype(jnp.bfloat16) for which_basis in range(BASES)]
    return jnp.stack(basis_list, axis=1)


def combine_bases(tile_set, source, radial_weight):
    per_basis = jnp.einsum("cbij,ckj->cbki", tile_set.astype(jnp.float32), source.astype(jnp.float32), precision=lax.Precision.HIGHEST)
    return jnp.einsum("cbki,bk->cki", per_basis, radial_weight, precision=lax.Precision.HIGHEST)


def gather_messages(source, positions, valid_atom, mask_float, radial_weight):
    running = jnp.zeros(source.shape, jnp.float32)
    for direction, (shift_x, shift_y, shift_z) in enumerate(offsets()):
        def shifted(values):
            return jnp.roll(values, (-shift_x, -shift_y, -shift_z), axis=(0, 1, 2))

        cell_gate = mask_float[..., direction] * shifted(mask_float)[..., 26 - direction]
        shift_vec = jnp.array([shift_x, shift_y, shift_z], jnp.float32)
        self_flag = jnp.float32(1.0 if direction == 13 else 0.0)

        def one_slab(members):
            own_pos, own_valid, other_pos, other_valid, slab_gate, slab_source = members
            cell_total = own_pos.shape[0] * own_pos.shape[1]
            tile_set = build_tiles(own_pos.reshape((cell_total,) + own_pos.shape[2:]), own_valid.reshape((cell_total,) + own_valid.shape[2:]), other_pos.reshape((cell_total,) + other_pos.shape[2:]), other_valid.reshape((cell_total,) + other_valid.shape[2:]), slab_gate.reshape(cell_total), shift_vec, self_flag)
            result = combine_bases(tile_set, slab_source.reshape((cell_total,) + slab_source.shape[2:]), radial_weight)
            return result.reshape(slab_source.shape)

        running = running + lax.map(one_slab, (positions, valid_atom, shifted(positions), shifted(valid_atom), cell_gate, shifted(source)))
    return running


def reference(features, cotangent, positions, counts, neighbour_mask, proj_weight, out_weight, radial_weight):
    highest = lax.Precision.HIGHEST
    valid_atom = (jnp.arange(ATOMS, dtype=jnp.int32)[None, None, None, :] < counts[..., None]).astype(jnp.float32)
    mask_float = neighbour_mask.astype(jnp.float32)
    projected = jnp.einsum("xyzin,nk->xyzki", features.astype(jnp.float32), proj_weight.astype(jnp.float32), precision=highest).astype(jnp.bfloat16)
    message = gather_messages(projected, positions, valid_atom, mask_float, radial_weight)
    activated = jax.nn.silu(message).astype(jnp.bfloat16)
    updated = (features.astype(jnp.float32) + jnp.einsum("xyzki,kn->xyzin", activated.astype(jnp.float32), out_weight.astype(jnp.float32), precision=highest)).astype(jnp.bfloat16)
    grad_act = jnp.einsum("xyzin,kn->xyzki", cotangent.astype(jnp.float32), out_weight.astype(jnp.float32), precision=highest)
    sigmoid_m = jax.nn.sigmoid(message)
    grad_msg = (grad_act * sigmoid_m * (1.0 + message * (1.0 - sigmoid_m))).astype(jnp.bfloat16)
    grad_proj = gather_messages(grad_msg, positions, valid_atom, mask_float, radial_weight).astype(jnp.bfloat16)
    feature_grad = (cotangent.astype(jnp.float32) + jnp.einsum("xyzki,nk->xyzin", grad_proj.astype(jnp.float32), proj_weight.astype(jnp.float32), precision=highest)).astype(jnp.bfloat16)
    return updated, feature_grad
```

```python
import functools

import jax
import jax.numpy as jnp
from jax import lax
from jax.experimental import pallas as pl
from jax.experimental.pallas import tpu as pltpu
from jax.sharding import PartitionSpec as P

MESH = pl.DeviceIdType.MESH
AXES = ("xy", "gz")
CENTRE = 4
GROUPS = ((4,), (1, 7), (3, 5), (0, 2), (6, 8))
SLOT = {n: at for at, n in enumerate(n for group in GROUPS for n in group)}
F32 = jnp.float32
BF16 = jnp.bfloat16


def nt(a, b):
    return lax.dot_general(a, b, (((1,), (1,)), ((), ())), preferred_element_type=F32)


def tn(a, b):
    return lax.dot_general(a, b, (((0,), (0,)), ((), ())), preferred_element_type=F32)


def direction(column, oy):
    return column // 3 * 9 + (oy + 1) * 3 + column % 3


def kernel(
    atoms,
    bases,
    feat_ref,
    cot_ref,
    pos_ref,
    counts_ref,
    mask_ref,
    proj_ref,
    outw_ref,
    radial_ref,
    updated_ref,
    grad_ref,
    packet_out,
    packet_in,
    own_cols,
    tiles,
    source,
    grads,
    send_sem,
    recv_sem,
):
    rows = feat_ref.shape[0]
    sizes = [lax.axis_size(axis) for axis in AXES]
    here = [lax.axis_index(axis) for axis in AXES]
    others = [n for group in GROUPS for n in group if n != CENTRE]

    def device_at(column):
        ox, oz = column // 3 - 1, column % 3 - 1
        return (lax.rem(here[0] + ox + sizes[0], sizes[0]), lax.rem(here[1] + oz + sizes[1], sizes[1]))

    barrier = pltpu.get_barrier_semaphore()
    for n in others:
        pl.semaphore_signal(barrier, inc=1, device_id=device_at(n), device_id_type=MESH)

    lane = lax.broadcasted_iota(jnp.int32, (1, rows), 1)
    upper = lane >= atoms
    valid_lane = (lane - jnp.where(upper, atoms, 0)) < jnp.where(upper, counts_ref[1], counts_ref[0])
    valid_row = valid_lane.astype(F32)

    def lanes_of(n):
        return pl.ds(SLOT[n] * rows, rows)

    projected = lax.dot_general(
        proj_ref[...], feat_ref[...], (((0,), (1,)), ((), ())), preferred_element_type=F32
    )
    source[:, lanes_of(CENTRE)] = (projected * valid_row).astype(BF16)

    place = 2.0 * jnp.concatenate([pos_ref[0], pos_ref[1]], axis=-1)
    for m in range(9):
        listed = [
            jnp.where(
                upper,
                mask_ref[1, direction(m, -oy)].astype(F32),
                mask_ref[0, direction(m, -oy)].astype(F32),
            )
            for oy in (-1, 0, 1)
        ]
        packet = jnp.concatenate([place] + listed + [jnp.zeros((2, rows), F32)], axis=0)
        packet_out[m] = packet
        if m == CENTRE:
            packet_in[CENTRE] = packet
            columns = packet.T
            for axis in range(3):
                own_cols[axis] = jnp.broadcast_to(columns[:, axis : axis + 1], (rows, rows))

    def copies(kind):
        made = {}
        for m in others:
            n = 8 - m
            if kind == 0:
                src, dst = packet_out.at[m], packet_in.at[n]
            else:
                held = source if kind == 1 else grads
                src, dst = held.at[:, lanes_of(CENTRE)], held.at[:, lanes_of(n)]
            made[n] = pltpu.make_async_remote_copy(
                src_ref=src,
                dst_ref=dst,
                send_sem=send_sem.at[kind, n],
                recv_sem=recv_sem.at[kind, n],
                device_id=device_at(m),
                device_id_type=MESH,
            )
        return made

    def build(n):
        ox, oz = n // 3 - 1, n % 3 - 1
        packet = packet_in[n]
        other_x = packet[0:1] + 2.0 * ox
        other_y = packet[1:2]
        other_z = packet[2:3] + 2.0 * oz
        chunk = 32
        for c in range(2):
            cross = upper if c == 0 else jnp.logical_not(upper)
            low, same, high = (
                packet[4 + oy : 5 + oy] * mask_ref[c, direction(n, oy)].astype(F32)
                for oy in (-1, 0, 1)
            )
            gate_low = jnp.where(cross, low, same)
            gate_high = jnp.where(cross, high, same)
            move_low = jnp.where(cross, -2.0, 0.0)
            move_high = jnp.where(cross, 2.0, 0.0)

            def part(step, carry):
                first = pl.multiple_of(c * atoms + step * chunk, chunk)
                some = pl.ds(first, chunk)
                dx = other_x - own_cols[0, some, :]
                dy = other_y - own_cols[1, some, :]
                dz = other_z - own_cols[2, some, :]
                above = dy > 0.0
                dy = dy + jnp.where(above, move_low, move_high)
                gate = jnp.where(above, gate_low, gate_high)
                near = jnp.minimum(dx * dx + dy * dy + dz * dz, 1.0)
                room = 1.0 - near
                envelope = room * room * gate
                if n == CENTRE:
                    at_row = lax.broadcasted_iota(jnp.int32, (chunk, rows), 0) + first
                    at_lane = lax.broadcasted_iota(jnp.int32, (chunk, rows), 1)
                    envelope = jnp.where(at_row == at_lane, 0.0, envelope)
                half = bases // 2
                v = bases * near - half
                up = jnp.exp(2.0 * v)
                down = jnp.exp(-2.0 * v)
                middle = envelope * jnp.exp(-2.0 * (v * v) - 0.5)
                up2, down2 = up * up, down * down
                high_value, low_value = middle * up, middle * down
                for step_out in range(half):
                    if step_out:
                        fall = EXP_FALL[step_out]
                        high_value = high_value * (up2 * fall)
                        low_value = low_value * (down2 * fall)
                    for b, value in ((half + step_out, high_value), (half - 1 - step_out, low_value)):
                        tiles[b, some, lanes_of(n)] = value.astype(BF16)
                return carry

            lax.fori_loop(0, atoms // chunk, part, 0)

    def gathered(held, group, total):
        width = len(group) * rows
        span = pl.ds(SLOT[group[0]] * rows, width)
        stack = tiles[:, :, span].reshape(bases * rows, width)
        sums = nt(stack, held[:, span])
        for b in range(bases):
            term = sums[b * rows : (b + 1) * rows] * radial_ref[b : b + 1, :]
            total = term if total is None else total + term
        return total

    pl.semaphore_wait(barrier, len(others))
    packets = copies(0)
    sources = copies(1)
    for n in others:
        packets[8 - n].start()
    for n in others:
        sources[8 - n].start()

    build(CENTRE)
    message = gathered(source, GROUPS[0], None)
    grad_act = nt(outw_ref[...], cot_ref[...])
    for group in GROUPS[1:]:
        for n in group:
            packets[n].wait_recv()
            build(n)
    for group in GROUPS[1:]:
        for n in group:
            sources[n].wait_recv()
        message = gathered(source, group, message)

    message = message.T * valid_row
    gate = 1.0 / (1.0 + jnp.exp(-message))
    grad_msg = grad_act * gate * (1.0 + message * (1.0 - gate)) * valid_row
    grads[:, lanes_of(CENTRE)] = grad_msg.astype(BF16)
    returns = copies(2)
    for n in others:
        returns[8 - n].start()

    activated = (message * gate).astype(BF16)
    updated_ref[...] = (feat_ref[...].astype(F32) + tn(activated, outw_ref[...])).astype(BF16)

    total = gathered(grads, GROUPS[0], None)
    for group in GROUPS[1:]:
        for n in group:
            returns[n].wait_recv()
        total = gathered(grads, group, total)
    at_row = lax.broadcasted_iota(jnp.int32, total.shape, 0)
    in_upper = at_row >= atoms
    kept = (at_row - jnp.where(in_upper, atoms, 0)) < jnp.where(in_upper, counts_ref[1], counts_ref[0])
    grad_proj = jnp.where(kept, total, 0.0).astype(BF16)
    grad_ref[...] = (cot_ref[...].astype(F32) + nt(grad_proj, proj_ref[...])).astype(BF16)

    for made in (packets, sources, returns):
        for n in others:
            made[n].wait_send()


EXP_FALL = [2.718281828459045 ** (-4.0 * step) for step in range(8)]


def on_device(
    features, cotangent, positions, counts, neighbour_mask, proj_weight, out_weight, radial_weight
):
    shape = features.shape
    cells, atoms, channels = shape[1], shape[3], shape[4]
    bases, width = radial_weight.shape
    rows = cells * atoms
    assert shape[0] == 1 and shape[2] == 1 and cells == 2
    vmem = pl.BlockSpec(memory_space=pltpu.VMEM)
    smem = pl.BlockSpec(memory_space=pltpu.SMEM)
    updated, grad = pl.pallas_call(
        functools.partial(kernel, atoms, bases),
        out_shape=[jax.ShapeDtypeStruct((rows, channels), BF16)] * 2,
        in_specs=[vmem, vmem, vmem, smem, smem, vmem, vmem, vmem],
        out_specs=[vmem, vmem],
        scratch_shapes=[
            pltpu.VMEM((9, 8, rows), F32),
            pltpu.VMEM((9, 8, rows), F32),
            pltpu.VMEM((3, rows, rows), F32),
            pltpu.VMEM((bases, rows, 9 * rows), BF16),
            pltpu.VMEM((width, 9 * rows), BF16),
            pltpu.VMEM((width, 9 * rows), BF16),
            pltpu.SemaphoreType.DMA((3, 9)),
            pltpu.SemaphoreType.DMA((3, 9)),
        ],
        compiler_params=pltpu.CompilerParams(collective_id=0, has_side_effects=True),
    )(
        features.reshape(rows, channels),
        cotangent.reshape(rows, channels),
        positions.reshape(cells, 3, atoms),
        counts.reshape(cells),
        neighbour_mask.reshape(cells, neighbour_mask.shape[-1]),
        proj_weight,
        out_weight,
        radial_weight,
    )
    return updated.reshape(shape), grad.reshape(shape)


def solution(mesh):
    cell = P("xy", None, "gz", None, None)
    return jax.shard_map(
        on_device,
        mesh=mesh,
        in_specs=(cell, cell, cell, P("xy", None, "gz"), P("xy", None, "gz", None), P(), P(), P()),
        out_specs=(cell, cell),
        check_vma=False,
    )
```

```python
import functools

import jax
import jax.numpy as jnp
from jax import lax
from jax.experimental import pallas as pl
from jax.experimental.pallas import tpu as pltpu
from jax.sharding import PartitionSpec as P

MESH = pl.DeviceIdType.MESH
AXES = ("xy", "gz")
GROUPS = (((0, 0),), ((-1, 0), (1, 0)), ((0, -1), (0, 1)), ((-1, -1), (-1, 1)), ((1, -1), (1, 1)))
SLOT = {at: slot for slot, at in enumerate(at for group in GROUPS for at in group)}
F32 = jnp.float32
BF16 = jnp.bfloat16


def nt(a, b):
    return lax.dot_general(a, b, (((1,), (1,)), ((), ())), preferred_element_type=F32)


def tn(a, b):
    return lax.dot_general(a, b, (((0,), (0,)), ((), ())), preferred_element_type=F32)


def direction(ox, oy, oz):
    return (ox + 1) * 9 + (oy + 1) * 3 + oz + 1


def kernel(
    atoms,
    bases,
    feat_hbm,
    cot_hbm,
    pos_hbm,
    counts_hbm,
    mask_hbm,
    proj_hbm,
    outw_hbm,
    radial_hbm,
    updated_hbm,
    grad_hbm,
    feat_ref,
    cot_ref,
    pos_ref,
    counts_ref,
    mask_ref,
    proj_ref,
    outw_ref,
    radial_ref,
    updated_ref,
    grad_ref,
    packet_out,
    packet_in,
    own_cols,
    tiles,
    source,
    grads,
    local_sem,
    send_sem,
    recv_sem,
):
    rows = feat_ref.shape[0]
    sizes = [lax.axis_size(axis) for axis in AXES]
    here = [lax.axis_index(axis) for axis in AXES]

    def device_at(ox, oz):
        return (lax.rem(here[0] + ox + sizes[0], sizes[0]), lax.rem(here[1] + oz + sizes[1], sizes[1]))

    barrier = pltpu.get_barrier_semaphore()
    beside = ((0, -1), (0, 1), (-1, 0), (1, 0))
    for ox, oz in beside:
        pl.semaphore_signal(barrier, inc=1, device_id=device_at(ox, oz), device_id_type=MESH)

    fetches = [
        pltpu.make_async_copy(far, near, local_sem.at[at])
        for at, (far, near) in enumerate(
            (
                (mask_hbm, mask_ref),
                (counts_hbm, counts_ref),
                (pos_hbm, pos_ref),
                (proj_hbm, proj_ref),
                (feat_hbm, feat_ref),
                (radial_hbm, radial_ref),
                (outw_hbm, outw_ref),
                (cot_hbm, cot_ref),
            )
        )
    ]
    for fetch in fetches:
        fetch.start()
    for fetch in fetches[:5]:
        fetch.wait()

    lane = lax.broadcasted_iota(jnp.int32, (1, rows), 1)
    upper = lane >= atoms
    valid_lane = (lane - jnp.where(upper, atoms, 0)) < jnp.where(upper, counts_ref[1], counts_ref[0])
    valid_row = valid_lane.astype(F32)

    def lanes_of(slot):
        first = slot * rows
        return pl.ds(first if isinstance(slot, int) else pl.multiple_of(first, rows), rows)

    place = 2.0 * jnp.concatenate(
        [
            jnp.concatenate([pos_ref[axis], pos_ref[3 + axis]], axis=-1)
            for axis in range(3)
        ],
        axis=0,
    )
    for oz in (-1, 0, 1):
        listed = [
            jnp.where(
                upper,
                mask_ref[1, direction(ox, -oy, oz)].astype(F32),
                mask_ref[0, direction(ox, -oy, oz)].astype(F32),
            )
            for ox in (-1, 0, 1)
            for oy in (-1, 0, 1)
        ]
        packet = jnp.concatenate([place] + listed + [jnp.zeros((4, rows), F32)], axis=0)
        packet_out[oz + 1] = packet
        if oz == 0:
            packet_in[0] = packet
    columns = jnp.concatenate([place, jnp.zeros((5, rows), F32)], axis=0).T
    for axis in range(3):
        own_cols[axis] = jnp.broadcast_to(columns[:, axis : axis + 1], (rows, rows))

    projected = nt(proj_ref[...], feat_ref[...])
    source[:, lanes_of(0)] = (projected * valid_row).astype(BF16)

    def held_at(kind, slot):
        if kind == 0:
            return packet_in.at[slot]
        return (source if kind == 1 else grads).at[:, lanes_of(slot)]

    def send(kind, src, slot, ox, oz):
        return pltpu.make_async_remote_copy(
            src_ref=src,
            dst_ref=held_at(kind, slot),
            send_sem=send_sem.at[kind, slot],
            recv_sem=recv_sem.at[kind, slot],
            device_id=device_at(ox, oz),
            device_id_type=MESH,
        )

    started = []

    def spread(kind):
        for ox, oz in beside:
            src = packet_out.at[oz + 1] if kind == 0 else held_at(kind, 0)
            copy = send(kind, src, SLOT[-ox, -oz], ox, oz)
            copy.start()
            started.append(copy)

    def arrived(kind, slot):
        send(kind, held_at(kind, slot), slot, 1, 0).wait_recv()

    def forward(kind, at):
        arrived(kind, 3 + at)
        for ox in (-1, 1):
            copy = send(kind, held_at(kind, 3 + at), SLOT[-ox, -1] + at, ox, 0)
            copy.start()
            started.append(copy)

    sooner = jnp.where(here[1] == 0, 1, 0)
    later = 1 - sooner

    def build(ox, oz):
        slot = SLOT[ox, oz]
        packet = packet_in[slot]
        other_x = packet[0:1] + 2.0 * ox
        other_y = packet[1:2]
        other_z = packet[2:3] + 2.0 * oz
        middle_row = 7 - 3 * ox
        chunk = 32
        for c in range(2):
            cross = upper if c == 0 else jnp.logical_not(upper)
            low, same, high = (
                packet[middle_row + oy : middle_row + oy + 1]
                * mask_ref[c, direction(ox, oy, oz)].astype(F32)
                for oy in (-1, 0, 1)
            )
            gate_low = jnp.where(cross, low, same)
            gate_high = jnp.where(cross, high, same)
            move_low = jnp.where(cross, -2.0, 0.0)
            move_high = jnp.where(cross, 2.0, 0.0)

            def part(step, carry):
                first = pl.multiple_of(c * atoms + step * chunk, chunk)
                some = pl.ds(first, chunk)
                dx = other_x - own_cols[0, some, :]
                dy = other_y - own_cols[1, some, :]
                dz = other_z - own_cols[2, some, :]
                above = dy > 0.0
                dy = dy + jnp.where(above, move_low, move_high)
                gate = jnp.where(above, gate_low, gate_high)
                near = jnp.minimum(dx * dx + dy * dy + dz * dz, 1.0)
                room = 1.0 - near
                envelope = room * room * gate
                if slot == 0:
                    at_row = lax.broadcasted_iota(jnp.int32, (chunk, rows), 0) + first
                    at_lane = lax.broadcasted_iota(jnp.int32, (chunk, rows), 1)
                    envelope = jnp.where(at_row == at_lane, 0.0, envelope)
                half = bases // 2
                v = bases * near - half
                up = jnp.exp(2.0 * v)
                down = jnp.exp(-2.0 * v)
                middle = envelope * jnp.exp(-2.0 * (v * v) - 0.5)
                up2, down2 = up * up, down * down
                high_value, low_value = middle * up, middle * down
                for step_out in range(half):
                    if step_out:
                        fall = EXP_FALL[step_out]
                        high_value = high_value * (up2 * fall)
                        low_value = low_value * (down2 * fall)
                    for b, value in ((half + step_out, high_value), (half - 1 - step_out, low_value)):
                        tiles[b, some, lanes_of(slot)] = value.astype(BF16)
                return carry

            lax.fori_loop(0, atoms // chunk, part, 0)

    def gathered(held, group, total):
        width = len(group) * rows
        span = pl.ds(SLOT[group[0]] * rows, width)
        stack = tiles[:, :, span].reshape(bases * rows, width)
        sums = nt(stack, held[:, span])
        for b in range(bases):
            term = sums[b * rows : (b + 1) * rows] * radial_ref[b : b + 1, :]
            total = term if total is None else total + term
        return total

    pl.semaphore_wait(barrier, len(beside))
    spread(0)
    spread(1)

    for fetch in fetches[5:]:
        fetch.wait()
    build(0, 0)
    message = gathered(source, GROUPS[0], None)
    grad_act = nt(outw_ref[...], cot_ref[...])
    forward(0, sooner)
    forward(1, sooner)
    for at in GROUPS[1]:
        arrived(0, SLOT[at])
        build(*at)
    for at in GROUPS[1]:
        arrived(1, SLOT[at])
    message = gathered(source, GROUPS[1], message)
    forward(0, later)
    forward(1, later)
    for at in GROUPS[2]:
        build(*at)
    message = gathered(source, GROUPS[2], message)
    for group in GROUPS[3:]:
        for at in group:
            arrived(0, SLOT[at])
            build(*at)
    for group in GROUPS[3:]:
        for at in group:
            arrived(1, SLOT[at])
        message = gathered(source, group, message)

    message = message.T * valid_row
    gate = 1.0 / (1.0 + jnp.exp(-message))
    grad_msg = grad_act * gate * (1.0 + message * (1.0 - gate)) * valid_row
    grads[:, lanes_of(0)] = grad_msg.astype(BF16)
    spread(2)

    activated = (message * gate).astype(BF16)
    updated_ref[...] = (feat_ref[...].astype(F32) + tn(activated, outw_ref[...])).astype(BF16)
    put_updated = pltpu.make_async_copy(updated_ref, updated_hbm, local_sem.at[8])
    put_updated.start()

    total = gathered(grads, GROUPS[0], None)
    forward(2, sooner)
    for at in GROUPS[1]:
        arrived(2, SLOT[at])
    total = gathered(grads, GROUPS[1], total)
    forward(2, later)
    for group in GROUPS[2:]:
        if group != GROUPS[2]:
            for at in group:
                arrived(2, SLOT[at])
        total = gathered(grads, group, total)
    at_row = lax.broadcasted_iota(jnp.int32, total.shape, 0)
    in_upper = at_row >= atoms
    kept = (at_row - jnp.where(in_upper, atoms, 0)) < jnp.where(in_upper, counts_ref[1], counts_ref[0])
    grad_proj = jnp.where(kept, total, 0.0).astype(BF16)
    pulled = jnp.dot(grad_proj, proj_ref[...], preferred_element_type=F32)
    grad_ref[...] = (cot_ref[...].astype(F32) + pulled).astype(BF16)
    put_grad = pltpu.make_async_copy(grad_ref, grad_hbm, local_sem.at[9])
    put_grad.start()

    for copy in started:
        copy.wait_send()
    put_updated.wait()
    put_grad.wait()


EXP_FALL = [2.718281828459045 ** (-4.0 * step) for step in range(8)]


def on_device(
    features, cotangent, positions, counts, neighbour_mask, proj_weight, out_weight, radial_weight
):
    shape = features.shape
    cells, atoms, channels = shape[1], shape[3], shape[4]
    bases, width = radial_weight.shape
    rows = cells * atoms
    assert shape[0] == 1 and shape[2] == 1 and cells == 2
    operands = (
        features.reshape(rows, channels),
        cotangent.reshape(rows, channels),
        positions.reshape(cells * 3, 1, atoms),
        counts.reshape(cells),
        neighbour_mask.reshape(cells, neighbour_mask.shape[-1]),
        proj_weight.T,
        out_weight,
        radial_weight,
    )
    held = [pltpu.SMEM if at in (3, 4) else pltpu.VMEM for at in range(len(operands))]
    updated, grad = pl.pallas_call(
        functools.partial(kernel, atoms, bases),
        out_shape=[jax.ShapeDtypeStruct((rows, channels), BF16)] * 2,
        in_specs=[pl.BlockSpec(memory_space=pl.ANY)] * len(operands),
        out_specs=[pl.BlockSpec(memory_space=pl.ANY)] * 2,
        scratch_shapes=[space(x.shape, x.dtype) for space, x in zip(held, operands)]
        + [
            pltpu.VMEM((rows, channels), BF16),
            pltpu.VMEM((rows, channels), BF16),
            pltpu.VMEM((3, 16, rows), F32),
            pltpu.VMEM((9, 16, rows), F32),
            pltpu.VMEM((3, rows, rows), F32),
            pltpu.VMEM((bases, rows, 9 * rows), BF16),
            pltpu.VMEM((width, 9 * rows), BF16),
            pltpu.VMEM((width, 9 * rows), BF16),
            pltpu.SemaphoreType.DMA((10,)),
            pltpu.SemaphoreType.DMA((3, 9)),
            pltpu.SemaphoreType.DMA((3, 9)),
        ],
        compiler_params=pltpu.CompilerParams(collective_id=0, has_side_effects=True),
    )(*operands)
    return updated.reshape(shape), grad.reshape(shape)


def solution(mesh):
    cell = P("xy", None, "gz", None, None)
    return jax.shard_map(
        on_device,
        mesh=mesh,
        in_specs=(cell, cell, cell, P("xy", None, "gz"), P("xy", None, "gz", None), P(), P(), P()),
        out_specs=(cell, cell),
        check_vma=False,
    )
```

```python
import functools

import jax
import jax.numpy as jnp
from jax import lax
from jax.experimental import pallas as pl
from jax.experimental.pallas import tpu as pltpu
from jax.sharding import PartitionSpec as P

MESH = pl.DeviceIdType.MESH
AXES = ("xy", "gz")
GROUPS = (((0, 0),), ((-1, 0), (1, 0)), ((0, -1), (0, 1)), ((-1, -1), (-1, 1)), ((1, -1), (1, 1)))
SLOT = {at: slot for slot, at in enumerate(at for group in GROUPS for at in group)}
F32 = jnp.float32
BF16 = jnp.bfloat16


def nt(a, b):
    return lax.dot_general(a, b, (((1,), (1,)), ((), ())), preferred_element_type=F32)


def tn(a, b):
    return lax.dot_general(a, b, (((0,), (0,)), ((), ())), preferred_element_type=F32)


def direction(ox, oy, oz):
    return (ox + 1) * 9 + (oy + 1) * 3 + oz + 1


def kernel(
    atoms,
    bases,
    feat_hbm,
    cot_hbm,
    pos_hbm,
    counts_hbm,
    mask_hbm,
    proj_hbm,
    outw_hbm,
    radial_hbm,
    updated_ref,
    grad_ref,
    feat_ref,
    cot_ref,
    pos_ref,
    counts_ref,
    mask_ref,
    proj_ref,
    outw_ref,
    radial_ref,
    packet_out,
    packet_in,
    own_cols,
    tiles,
    source,
    grads,
    local_sem,
    send_sem,
    recv_sem,
):
    rows = feat_ref.shape[0]
    sizes = [lax.axis_size(axis) for axis in AXES]
    here = [lax.axis_index(axis) for axis in AXES]

    def device_at(ox, oz):
        return (lax.rem(here[0] + ox + sizes[0], sizes[0]), lax.rem(here[1] + oz + sizes[1], sizes[1]))

    barrier = pltpu.get_barrier_semaphore()
    others = [at for at, slot in SLOT.items() if slot]
    for ox, oz in others[::-1]:
        pl.semaphore_signal(barrier, inc=1, device_id=device_at(ox, oz), device_id_type=MESH)

    fetches = [
        pltpu.make_async_copy(far, near, local_sem.at[at])
        for at, (far, near) in enumerate(
            (
                (mask_hbm, mask_ref),
                (counts_hbm, counts_ref),
                (pos_hbm, pos_ref),
                (proj_hbm, proj_ref),
                (feat_hbm, feat_ref),
                (radial_hbm, radial_ref),
                (outw_hbm, outw_ref),
                (cot_hbm, cot_ref),
            )
        )
    ]
    for fetch in fetches:
        fetch.start()
    for fetch in fetches[:5]:
        fetch.wait()

    lane = lax.broadcasted_iota(jnp.int32, (1, rows), 1)
    upper = lane >= atoms
    valid_lane = (lane - jnp.where(upper, atoms, 0)) < jnp.where(upper, counts_ref[1], counts_ref[0])
    valid_row = valid_lane.astype(F32)

    def lanes_of(slot):
        first = slot * rows
        return pl.ds(first if isinstance(slot, int) else pl.multiple_of(first, rows), rows)

    place = 2.0 * jnp.concatenate(
        [
            jnp.concatenate([pos_ref[axis], pos_ref[3 + axis]], axis=-1)
            for axis in range(3)
        ],
        axis=0,
    )
    for (ox, oz), slot in SLOT.items():
        listed = [
            jnp.where(
                upper,
                mask_ref[1, direction(ox, -oy, oz)].astype(F32),
                mask_ref[0, direction(ox, -oy, oz)].astype(F32),
            )
            for oy in (-1, 0, 1)
        ]
        packet = jnp.concatenate([place] + listed + [jnp.zeros((2, rows), F32)], axis=0)
        packet_out[slot] = packet
        if slot == 0:
            packet_in[0] = packet
    columns = jnp.concatenate([place, jnp.zeros((5, rows), F32)], axis=0).T
    for axis in range(3):
        own_cols[axis] = jnp.broadcast_to(columns[:, axis : axis + 1], (rows, rows))

    projected = nt(proj_ref[...], feat_ref[...])
    source[:, lanes_of(0)] = (projected * valid_row).astype(BF16)

    def held_at(kind, slot):
        if kind == 0:
            return packet_in.at[slot]
        return (source if kind == 1 else grads).at[:, lanes_of(slot)]

    def send(kind, src, slot, ox, oz):
        return pltpu.make_async_remote_copy(
            src_ref=src,
            dst_ref=held_at(kind, slot),
            send_sem=send_sem.at[kind, slot],
            recv_sem=recv_sem.at[kind, slot],
            device_id=device_at(ox, oz),
            device_id_type=MESH,
        )

    started = []

    def spread(kind):
        for ox, oz in others:
            src = packet_out.at[SLOT[ox, oz]] if kind == 0 else held_at(kind, 0)
            copy = send(kind, src, SLOT[-ox, -oz], ox, oz)
            copy.start()
            started.append(copy)

    def arrived(kind, slot):
        send(kind, held_at(kind, slot), slot, 1, 0).wait_recv()

    def build(ox, oz):
        slot = SLOT[ox, oz]
        packet = packet_in[slot]
        other_x = packet[0:1] + 2.0 * ox
        other_y = packet[1:2]
        other_z = packet[2:3] + 2.0 * oz
        middle_row = 4
        chunk = 32
        for c in range(2):
            cross = upper if c == 0 else jnp.logical_not(upper)
            low, same, high = (
                packet[middle_row + oy : middle_row + oy + 1]
                * mask_ref[c, direction(ox, oy, oz)].astype(F32)
                for oy in (-1, 0, 1)
            )
            gate_low = jnp.where(cross, low, same)
            gate_high = jnp.where(cross, high, same)
            move_low = jnp.where(cross, -2.0, 0.0)
            move_high = jnp.where(cross, 2.0, 0.0)

            def part(step, carry):
                first = pl.multiple_of(c * atoms + step * chunk, chunk)
                some = pl.ds(first, chunk)
                dx = other_x - own_cols[0, some, :]
                dy = other_y - own_cols[1, some, :]
                dz = other_z - own_cols[2, some, :]
                above = dy > 0.0
                dy = dy + jnp.where(above, move_low, move_high)
                gate = jnp.where(above, gate_low, gate_high)
                near = jnp.minimum(dx * dx + dy * dy + dz * dz, 1.0)
                room = 1.0 - near
                envelope = room * room * gate
                if slot == 0:
                    at_row = lax.broadcasted_iota(jnp.int32, (chunk, rows), 0) + first
                    at_lane = lax.broadcasted_iota(jnp.int32, (chunk, rows), 1)
                    envelope = jnp.where(at_row == at_lane, 0.0, envelope)
                half = bases // 2
                v = bases * near - half
                up = jnp.exp(2.0 * v)
                down = jnp.exp(-2.0 * v)
                middle = envelope * jnp.exp(-2.0 * (v * v) - 0.5)
                up2, down2 = up * up, down * down
                high_value, low_value = middle * up, middle * down
                for step_out in range(half):
                    if step_out:
                        fall = EXP_FALL[step_out]
                        high_value = high_value * (up2 * fall)
                        low_value = low_value * (down2 * fall)
                    for b, value in ((half + step_out, high_value), (half - 1 - step_out, low_value)):
                        tiles[b, some, lanes_of(slot)] = value.astype(BF16)
                return carry

            lax.fori_loop(0, atoms // chunk, part, 0)

    def gathered(held, group, total):
        width = len(group) * rows
        span = pl.ds(SLOT[group[0]] * rows, width)
        stack = tiles[:, :, span].reshape(bases * rows, width)
        sums = nt(stack, held[:, span])
        for b in range(bases):
            term = sums[b * rows : (b + 1) * rows] * radial_ref[b : b + 1, :]
            total = term if total is None else total + term
        return total

    pl.semaphore_wait(barrier, len(others))
    spread(0)
    spread(1)

    for fetch in fetches[5:]:
        fetch.wait()
    build(0, 0)
    message = gathered(source, GROUPS[0], None)
    grad_act = nt(outw_ref[...], cot_ref[...])
    for group in GROUPS[1:]:
        for at in group:
            arrived(0, SLOT[at])
            build(*at)
        for at in group:
            arrived(1, SLOT[at])
        message = gathered(source, group, message)

    message = message.T * valid_row
    gate = 1.0 / (1.0 + jnp.exp(-message))
    grad_msg = grad_act * gate * (1.0 + message * (1.0 - gate)) * valid_row
    grads[:, lanes_of(0)] = grad_msg.astype(BF16)
    spread(2)

    activated = (message * gate).astype(BF16)
    updated_ref[...] = (feat_ref[...].astype(F32) + tn(activated, outw_ref[...])).astype(BF16)

    total = gathered(grads, GROUPS[0], None)
    for group in GROUPS[1:]:
        for at in group:
            arrived(2, SLOT[at])
        total = gathered(grads, group, total)
    at_row = lax.broadcasted_iota(jnp.int32, total.shape, 0)
    in_upper = at_row >= atoms
    kept = (at_row - jnp.where(in_upper, atoms, 0)) < jnp.where(in_upper, counts_ref[1], counts_ref[0])
    grad_proj = jnp.where(kept, total, 0.0).astype(BF16)
    pulled = jnp.dot(grad_proj, proj_ref[...], preferred_element_type=F32)
    grad_ref[...] = (cot_ref[...].astype(F32) + pulled).astype(BF16)

    for copy in started:
        copy.wait_send()


EXP_FALL = [2.718281828459045 ** (-4.0 * step) for step in range(8)]


def on_device(
    features, cotangent, positions, counts, neighbour_mask, proj_weight, out_weight, radial_weight
):
    shape = features.shape
    cells, atoms, channels = shape[1], shape[3], shape[4]
    bases, width = radial_weight.shape
    rows = cells * atoms
    assert shape[0] == 1 and shape[2] == 1 and cells == 2
    operands = (
        features.reshape(rows, channels),
        cotangent.reshape(rows, channels),
        positions.reshape(cells * 3, 1, atoms),
        counts.reshape(cells),
        neighbour_mask.reshape(cells, neighbour_mask.shape[-1]),
        proj_weight.T,
        out_weight,
        radial_weight,
    )
    held = [pltpu.SMEM if at in (3, 4) else pltpu.VMEM for at in range(len(operands))]
    updated, grad = pl.pallas_call(
        functools.partial(kernel, atoms, bases),
        out_shape=[pltpu.VMEM((rows, channels), BF16)] * 2,
        in_specs=[pl.BlockSpec(memory_space=pl.ANY)] * len(operands),
        out_specs=[pl.BlockSpec(memory_space=pltpu.VMEM)] * 2,
        scratch_shapes=[space(x.shape, x.dtype) for space, x in zip(held, operands)]
        + [
            pltpu.VMEM((9, 8, rows), F32),
            pltpu.VMEM((9, 8, rows), F32),
            pltpu.VMEM((3, rows, rows), F32),
            pltpu.VMEM((bases, rows, 9 * rows), BF16),
            pltpu.VMEM((width, 9 * rows), BF16),
            pltpu.VMEM((width, 9 * rows), BF16),
            pltpu.SemaphoreType.DMA((10,)),
            pltpu.SemaphoreType.DMA((3, 9)),
            pltpu.SemaphoreType.DMA((3, 9)),
        ],
        compiler_params=pltpu.CompilerParams(collective_id=0, has_side_effects=True),
    )(*operands)
    return updated.reshape(shape), grad.reshape(shape)


def solution(mesh):
    cell = P("xy", None, "gz", None, None)
    return jax.shard_map(
        on_device,
        mesh=mesh,
        in_specs=(cell, cell, cell, P("xy", None, "gz"), P("xy", None, "gz", None), P(), P(), P()),
        out_specs=(cell, cell),
        check_vma=False,
    )
```

```python
import functools

import jax
import jax.numpy as jnp
from jax import lax
from jax.experimental import pallas as pl
from jax.experimental.pallas import tpu as pltpu
from jax.sharding import PartitionSpec as P

MESH = pl.DeviceIdType.MESH
AXES = ("xy", "gz")
GROUPS = (((0, 0),), ((-1, 0), (1, 0)), ((0, -1), (-1, -1), (1, -1)), ((0, 1), (-1, 1), (1, 1)))
ORDER = ((-1, None), (1, None), (-1, True), (1, True), (-1, False), (1, False), (0, True), (0, False))
SLOT = {at: slot for slot, at in enumerate(at for group in GROUPS for at in group)}
F32 = jnp.float32
BF16 = jnp.bfloat16


def nt(a, b):
    return lax.dot_general(a, b, (((1,), (1,)), ((), ())), preferred_element_type=F32)


def tn(a, b):
    return lax.dot_general(a, b, (((0,), (0,)), ((), ())), preferred_element_type=F32)


def direction(ox, oy, oz):
    return (ox + 1) * 9 + (oy + 1) * 3 + oz + 1


def kernel(
    atoms,
    bases,
    feat_hbm,
    cot_hbm,
    pos_hbm,
    counts_hbm,
    mask_hbm,
    proj_hbm,
    outw_hbm,
    radial_hbm,
    both_ref,
    feat_ref,
    cot_ref,
    pos_ref,
    counts_ref,
    mask_ref,
    proj_ref,
    outw_ref,
    radial_ref,
    packet_out,
    packet_in,
    own_cols,
    tiles,
    source,
    grads,
    local_sem,
    send_sem,
    recv_sem,
):
    rows = feat_ref.shape[0]
    sizes = [lax.axis_size(axis) for axis in AXES]
    here = [lax.axis_index(axis) for axis in AXES]

    def device_at(ox, oz):
        return (lax.rem(here[0] + ox + sizes[0], sizes[0]), lax.rem(here[1] + oz + sizes[1], sizes[1]))

    sooner = jnp.where(here[1] == 0, 1, 0)
    later = 1 - sooner
    barrier = pltpu.get_barrier_semaphore()
    others = [(-1, 0), (1, 0), (-1, -1), (-1, 1), (1, -1), (1, 1), (0, -1), (0, 1)]
    for ox, oz in others[::-1]:
        pl.semaphore_signal(barrier, inc=1, device_id=device_at(ox, oz), device_id_type=MESH)

    fetches = [
        pltpu.make_async_copy(far, near, local_sem.at[at])
        for at, (far, near) in enumerate(
            (
                (mask_hbm, mask_ref),
                (counts_hbm, counts_ref),
                (pos_hbm, pos_ref),
                (proj_hbm, proj_ref),
                (feat_hbm, feat_ref),
                (radial_hbm, radial_ref),
                (outw_hbm, outw_ref),
                (cot_hbm, cot_ref),
            )
        )
    ]
    for fetch in fetches:
        fetch.start()
    for fetch in fetches[:3]:
        fetch.wait()

    lane = lax.broadcasted_iota(jnp.int32, (1, rows), 1)
    upper = lane >= atoms
    valid_lane = (lane - jnp.where(upper, atoms, 0)) < jnp.where(upper, counts_ref[1], counts_ref[0])
    valid_row = valid_lane.astype(F32)

    def lanes_of(slot):
        first = slot * rows
        return pl.ds(first if isinstance(slot, int) else pl.multiple_of(first, rows), rows)

    place = 2.0 * jnp.concatenate(
        [
            jnp.concatenate([pos_ref[axis], pos_ref[3 + axis]], axis=-1)
            for axis in range(3)
        ],
        axis=0,
    )
    for (ox, oz), slot in SLOT.items():
        listed = [
            jnp.where(
                upper,
                mask_ref[1, direction(ox, -oy, oz)].astype(F32),
                mask_ref[0, direction(ox, -oy, oz)].astype(F32),
            )
            for oy in (-1, 0, 1)
        ]
        packet = jnp.concatenate([place] + listed + [jnp.zeros((2, rows), F32)], axis=0)
        packet_out[slot] = packet
        if slot == 0:
            packet_in[0] = packet
    def held_at(kind, slot):
        if kind == 0:
            return packet_in.at[slot]
        return (source if kind == 1 else grads).at[:, lanes_of(slot)]

    def send(kind, src, slot, ox, oz):
        return pltpu.make_async_remote_copy(
            src_ref=src,
            dst_ref=held_at(kind, slot),
            send_sem=send_sem.at[kind, slot],
            recv_sem=recv_sem.at[kind, slot],
            device_id=device_at(ox, oz),
            device_id_type=MESH,
        )

    started = []

    def spread(kind):
        for ox, side in ORDER:
            if side is None:
                mine, theirs, oz = SLOT[ox, 0], SLOT[-ox, 0], 0
            else:
                which = later if side else sooner
                mine, theirs = SLOT[ox, -1] + 3 * which, SLOT[-ox, -1] + 3 * (1 - which)
                oz = 2 * which - 1
            src = packet_out.at[mine] if kind == 0 else held_at(kind, 0)
            copy = send(kind, src, theirs, ox, oz)
            copy.start()
            started.append(copy)

    def arrived(kind, slot):
        send(kind, held_at(kind, slot), slot, 1, 0).wait_recv()

    def build(ox, oz, slot):
        packet = packet_in[slot]
        other_x = packet[0:1] + 2.0 * ox
        other_y = packet[1:2]
        other_z = packet[2:3] + (2.0 * oz if isinstance(oz, int) else 2.0 * oz.astype(F32))
        middle_row = 4
        chunk = 32
        for c in range(2):
            cross = upper if c == 0 else jnp.logical_not(upper)
            low, same, high = (
                packet[middle_row + oy : middle_row + oy + 1]
                * mask_ref[c, direction(ox, oy, oz)].astype(F32)
                for oy in (-1, 0, 1)
            )
            gate_low = jnp.where(cross, low, same)
            gate_high = jnp.where(cross, high, same)
            move_low = jnp.where(cross, -2.0, 0.0)
            move_high = jnp.where(cross, 2.0, 0.0)

            def part(step, carry):
                first = pl.multiple_of(c * atoms + step * chunk, chunk)
                some = pl.ds(first, chunk)
                dx = other_x - own_cols[0, some, :]
                dy = other_y - own_cols[1, some, :]
                dz = other_z - own_cols[2, some, :]
                above = dy > 0.0
                dy = dy + jnp.where(above, move_low, move_high)
                gate = jnp.where(above, gate_low, gate_high)
                near = jnp.minimum(dx * dx + dy * dy + dz * dz, 1.0)
                room = 1.0 - near
                envelope = room * room * gate
                if isinstance(slot, int) and slot == 0:
                    at_row = lax.broadcasted_iota(jnp.int32, (chunk, rows), 0) + first
                    at_lane = lax.broadcasted_iota(jnp.int32, (chunk, rows), 1)
                    envelope = jnp.where(at_row == at_lane, 0.0, envelope)
                half = bases // 2
                v = bases * near - half
                up = jnp.exp(2.0 * v)
                down = jnp.exp(-2.0 * v)
                middle = envelope * jnp.exp(-2.0 * (v * v) - 0.5)
                up2, down2 = up * up, down * down
                high_value, low_value = middle * up, middle * down
                for step_out in range(half):
                    if step_out:
                        fall = EXP_FALL[step_out]
                        high_value = high_value * (up2 * fall)
                        low_value = low_value * (down2 * fall)
                    for b, value in ((half + step_out, high_value), (half - 1 - step_out, low_value)):
                        tiles[b, some, lanes_of(slot)] = value.astype(BF16)
                return carry

            lax.fori_loop(0, atoms // chunk, part, 0)

    def gathered(held, slot, count, total):
        width = count * rows
        first = slot * rows
        span = pl.ds(first if isinstance(slot, int) else pl.multiple_of(first, rows), width)
        stack = tiles[:, :, span].reshape(bases * rows, width)
        sums = nt(stack, held[:, span])
        for b in range(bases):
            term = sums[b * rows : (b + 1) * rows] * radial_ref[b : b + 1, :]
            total = term if total is None else total + term
        return total

    pl.semaphore_wait(barrier, len(others))
    spread(0)
    for fetch in fetches[3:5]:
        fetch.wait()
    projected = nt(proj_ref[...], feat_ref[...])
    source[:, lanes_of(0)] = (projected * valid_row).astype(BF16)
    spread(1)
    columns = jnp.concatenate([place, jnp.zeros((5, rows), F32)], axis=0).T
    for axis in range(3):
        own_cols[axis] = jnp.broadcast_to(columns[:, axis : axis + 1], (rows, rows))


    for fetch in fetches[5:]:
        fetch.wait()
    build(0, 0, 0)
    message = gathered(source, 0, 1, None)
    grad_act = nt(outw_ref[...], cot_ref[...])
    for at in GROUPS[1]:
        arrived(0, SLOT[at])
        build(*at, SLOT[at])
    for at in GROUPS[1]:
        arrived(1, SLOT[at])
    message = gathered(source, 1, 2, message)
    for which, oz in ((sooner, 2 * sooner - 1), (later, 2 * later - 1)):
        for at, ox in enumerate((0, -1, 1)):
            arrived(0, 3 + 3 * which + at)
            build(ox, oz, 3 + 3 * which + at)
        for at in range(3):
            arrived(1, 3 + 3 * which + at)
        message = gathered(source, 3 + 3 * which, 3, message)

    message = message.T * valid_row
    gate = 1.0 / (1.0 + jnp.exp(-message))
    grad_msg = grad_act * gate * (1.0 + message * (1.0 - gate)) * valid_row
    grads[:, lanes_of(0)] = grad_msg.astype(BF16)
    spread(2)

    activated = (message * gate).astype(BF16)
    both_ref[0] = (feat_ref[...].astype(F32) + tn(activated, outw_ref[...])).astype(BF16)

    total = gathered(grads, 0, 1, None)
    for at in (1, 2):
        arrived(2, at)
    total = gathered(grads, 1, 2, total)
    for which in (sooner, later):
        for at in range(3):
            arrived(2, 3 + 3 * which + at)
        total = gathered(grads, 3 + 3 * which, 3, total)
    at_row = lax.broadcasted_iota(jnp.int32, total.shape, 0)
    in_upper = at_row >= atoms
    kept = (at_row - jnp.where(in_upper, atoms, 0)) < jnp.where(in_upper, counts_ref[1], counts_ref[0])
    grad_proj = jnp.where(kept, total, 0.0).astype(BF16)
    pulled = jnp.dot(grad_proj, proj_ref[...], preferred_element_type=F32)
    both_ref[1] = (cot_ref[...].astype(F32) + pulled).astype(BF16)

    for copy in started:
        copy.wait_send()


EXP_FALL = [2.718281828459045 ** (-4.0 * step) for step in range(8)]


def on_device(
    features, cotangent, positions, counts, neighbour_mask, proj_weight, out_weight, radial_weight
):
    shape = features.shape
    cells, atoms, channels = shape[1], shape[3], shape[4]
    bases, width = radial_weight.shape
    rows = cells * atoms
    assert shape[0] == 1 and shape[2] == 1 and cells == 2
    operands = (
        features.reshape(rows, channels),
        cotangent.reshape(rows, channels),
        positions.reshape(cells * 3, 1, atoms),
        counts.reshape(cells),
        neighbour_mask.reshape(cells, neighbour_mask.shape[-1]),
        proj_weight.T,
        out_weight,
        radial_weight,
    )
    held = [pltpu.SMEM if at in (3, 4) else pltpu.VMEM for at in range(len(operands))]
    both = pl.pallas_call(
        functools.partial(kernel, atoms, bases),
        out_shape=pltpu.VMEM((2, rows, channels), BF16),
        in_specs=[pl.BlockSpec(memory_space=pl.ANY)] * len(operands),
        out_specs=pl.BlockSpec(memory_space=pltpu.VMEM),
        scratch_shapes=[space(x.shape, x.dtype) for space, x in zip(held, operands)]
        + [
            pltpu.VMEM((9, 8, rows), F32),
            pltpu.VMEM((9, 8, rows), F32),
            pltpu.VMEM((3, rows, rows), F32),
            pltpu.VMEM((bases, rows, 9 * rows), BF16),
            pltpu.VMEM((width, 9 * rows), BF16),
            pltpu.VMEM((width, 9 * rows), BF16),
            pltpu.SemaphoreType.DMA((10,)),
            pltpu.SemaphoreType.DMA((3, 9)),
            pltpu.SemaphoreType.DMA((3, 9)),
        ],
        compiler_params=pltpu.CompilerParams(collective_id=0, has_side_effects=True),
    )(*operands)
    return both[0].reshape(shape), both[1].reshape(shape)


def solution(mesh):
    cell = P("xy", None, "gz", None, None)
    return jax.shard_map(
        on_device,
        mesh=mesh,
        in_specs=(cell, cell, cell, P("xy", None, "gz"), P("xy", None, "gz", None), P(), P(), P()),
        out_specs=(cell, cell),
        check_vma=False,
    )
```
